32 devices in a mesh: img: 8 (over y, x, core), cls: 4 (over z).
Axes of the slice: x: 2, y: 2, z: 4, core: 2. Of those that a mesh axis runs over, the one named last changes fastest.
Arguments:
- images: bfloat16 [64, 9216], P('img'), may hold values from -64 to 64
- references: bfloat16 [512, 9216], P(('img', 'cls')), may hold values from -0.2 to 0.2
- class_logprior: bfloat16 [512], P(('img', 'cls')), may hold values from -3 to 3
- ctf_table: float32 [16, 32], replicated, may hold values from -1 to 1, as said below
- noise_power: float32 [32], replicated, may hold values from 0.5 to 2
- tau_power: float32 [32], replicated, may hold values from 0.5 to 4
- defocus: int32 [64], P('img'), may hold values from 0 to 15
- offsets: int32 [64, 4, 2], P('img'), may hold values from -3 to 3
Outputs:
- new_refs: float32 [512, 9216], P(('img', 'cls'))
- new_weights: float32 [512], P(('img', 'cls'))
- loglik: float32 [64], P('img')
The draws below stay inside these ranges and needn't reach their ends.
Inputs may be any that keep to these rules, and one draw needn't show every extreme that they name: `ctf_table`: each row is a contrast transfer curve that oscillates over the cycles.
All inputs are finite; a program needn't handle non-finite values.
Results may differ from the reference program's by a relative error of at most 0.0068.
Values may be sent and summed in bfloat16 or wider, within the bound.
A program may use at most 64 MiB of HBM per device.

```python
import math
import jax
import jax.numpy as jnp
from jax import lax

TRANS = 4
CYCLES = 32
ANG = 144
ROT = 36
K = 512
NDEF = 16
IMGS = 64


def draw_common(key):
    width = 2 * CYCLES * ANG
    keys = [jax.random.fold_in(key, 101 + number) for number in range(11)]
    refs = jnp.clip(jax.random.normal(keys[1], (K, width)) * 0.03, -0.2, 0.2)
    slope = jax.random.uniform(keys[2], (NDEF, 1), minval=0.002, maxval=0.02)
    radius = jnp.arange(CYCLES, dtype=jnp.float32) + 1.0
    curves = -jnp.sin(slope * radius[None, :] * radius[None, :] + 0.1)
    noise = jnp.exp(jax.random.uniform(keys[3], (CYCLES,), minval=math.log(0.5), maxval=math.log(2.0)))
    groups = jax.random.randint(keys[4], (IMGS,), 0, NDEF)
    shifts = jax.random.randint(keys[5], (IMGS, TRANS, 2), -3, 4)
    pictures = jnp.clip(jax.random.normal(keys[6], (IMGS, width)), -6.0, 6.0)
    return (refs, curves, noise, groups, shifts, pictures)


def draw_images(key, part):
    return draw_common(key)[5].astype(jnp.bfloat16)


def draw_references(key, part):
    return draw_common(key)[0].astype(jnp.bfloat16)


def draw_ctf_table(key, part):
    return draw_common(key)[1].astype(jnp.float32)


def draw_noise_power(key, part):
    return draw_common(key)[2].astype(jnp.float32)


def draw_defocus(key, part):
    return draw_common(key)[3].astype(jnp.int32)


def draw_offsets(key, part):
    return draw_common(key)[4].astype(jnp.int32)


def block_scale(own_key, shape, cuts, least, top_value):
    def one(dim, blocks):
        draws = jax.random.uniform(jax.random.fold_in(jax.random.fold_in(own_key, 6), dim), (blocks,), jnp.float32, least / len(cuts), top_value / len(cuts))
        return jnp.repeat(jnp.exp(draws), shape[dim] // blocks).reshape((-1,) + (1,) * (len(shape) - dim - 1))

    level = one(*cuts[0])
    for cut in cuts[1:]:
        level = level * one(*cut)
    return level


def gaussian(own_key, dims, scale, limit, pieces=(), kind=jnp.bfloat16):
    entries = scale * jax.random.normal(own_key, dims, jnp.float32)
    if pieces:
        entries = entries * block_scale(own_key, dims, pieces, -0.22, 0.18)
    return jnp.clip(entries, -limit, limit).astype(kind)


def setup_inputs(seed: int = 0) -> dict:
    splits = jax.random.split(jax.random.key(seed), 9)
    images = draw_images(jax.random.fold_in(splits[8], 71), 0)
    references = draw_references(jax.random.fold_in(splits[8], 71), 0)
    class_logprior = gaussian(splits[2], (K,), 0.5, 3.0, ((0, 32),))
    ctf_table = draw_ctf_table(jax.random.fold_in(splits[8], 71), 0)
    noise_power = draw_noise_power(jax.random.fold_in(splits[8], 71), 0)
    tau_power = jnp.clip(jnp.exp(jax.random.uniform(splits[5], (CYCLES,), jnp.float32, math.log(0.5), math.log(4.0))), 0.5, 4.0)
    defocus = draw_defocus(jax.random.fold_in(splits[8], 71), 0)
    offsets = draw_offsets(jax.random.fold_in(splits[8], 71), 0)
    return {"images": images, "references": references, "class_logprior": class_logprior, "ctf_table": ctf_table, "noise_power": noise_power, "tau_power": tau_power, "defocus": defocus, "offsets": offsets}


offset_sigma = 2.0


def phase_table(shift_x, shift_y):
    radius = jnp.arange(CYCLES, dtype=jnp.float32) + 1.0
    theta = 2.0 * math.pi * jnp.arange(ANG, dtype=jnp.float32) / ANG
    freq_x = radius[:, None] * jnp.cos(theta)[None, :]
    freq_y = radius[:, None] * jnp.sin(theta)[None, :]
    return -2.0 * math.pi * (shift_x[..., None, None] * freq_x + shift_y[..., None, None] * freq_y) / (2.0 * CYCLES)


def reference(images, references, class_logprior, ctf_table, noise_power, tau_power, defocus, offsets):
    width = 2 * CYCLES * ANG
    stride = ANG // ROT
    rows = IMGS * TRANS
    pixels = images.astype(jnp.float32).reshape(IMGS, 2, CYCLES, ANG)
    shift = offsets.astype(jnp.float32)
    angle = phase_table(shift[..., 0], shift[..., 1])
    cosine = jnp.cos(angle)
    sine = jnp.sin(angle)
    real_part = pixels[:, None, 0] * cosine - pixels[:, None, 1] * sine
    imag_part = pixels[:, None, 0] * sine + pixels[:, None, 1] * cosine
    shifted = jnp.stack([real_part, imag_part], axis=2)
    contrast = ctf_table[defocus]
    weighted = (shifted * (contrast / noise_power[None, :])[:, None, None, :, None]).astype(jnp.bfloat16).reshape(rows, width)
    inserted = (shifted * contrast[:, None, None, :, None]).astype(jnp.bfloat16).reshape(rows, width)
    norm_coef = contrast * contrast / (2.0 * noise_power[None, :])
    power = jnp.sum(jnp.square(references.astype(jnp.float32).reshape(K, 2, CYCLES, ANG)), axis=(1, 3))
    penalty = jnp.dot(norm_coef, power.T, precision=lax.Precision.HIGHEST)
    trans_prior = -(shift[..., 0] * shift[..., 0] + shift[..., 1] * shift[..., 1]) / (2.0 * offset_sigma * offset_sigma)

    def score_block(chosen):
        shaped = chosen.reshape(8, 2, CYCLES, ANG)
        rotated = jnp.stack([jnp.roll(shaped, stride * turn, axis=-1) for turn in range(ROT)], axis=1).reshape(8 * ROT, width)
        return lax.dot_general(weighted, rotated, (((1,), (1,)), ((), ())), preferred_element_type=jnp.float32)

    cross = lax.map(score_block, references.reshape(K // 8, 8, width))
    cross = cross.reshape(K // 8, rows, 8, ROT).transpose(1, 0, 2, 3).reshape(IMGS, TRANS, K, ROT)
    logp = cross - penalty[:, None, :, None] + class_logprior.astype(jnp.float32)[None, None, :, None]
    logp = logp + trans_prior[:, :, None, None]
    per_image = logp.reshape(IMGS, TRANS * K * ROT)
    peak = jnp.max(per_image, axis=1)
    total = jnp.sum(jnp.exp(per_image - peak[:, None]), axis=1)
    loglik = peak + jnp.log(total)
    posterior = (jnp.exp(per_image - peak[:, None]) / total[:, None]).astype(jnp.bfloat16).reshape(rows, K, ROT)

    def insert_block(section):
        product = lax.dot_general(section, inserted, (((0,), (0,)), ((), ())), preferred_element_type=jnp.float32)
        product = product.reshape(8, ROT, 2, CYCLES, ANG)
        collected = jnp.zeros((8, 2, CYCLES, ANG), jnp.float32)
        for turn in range(ROT):
            collected = collected + jnp.roll(product[:, turn], -stride * turn, axis=-1)
        return collected

    sections = posterior.reshape(rows, K // 8, 8 * ROT).transpose(1, 0, 2)
    numer = lax.map(insert_block, sections).reshape(K, 2, CYCLES, ANG)
    post_sum = jnp.sum(posterior.astype(jnp.float32), axis=2)
    squared_rows = jnp.repeat(contrast * contrast, TRANS, axis=0)
    denom = lax.dot_general(post_sum, squared_rows, (((0,), (0,)), ((), ())), precision=lax.Precision.HIGHEST)
    weight = jnp.sum(post_sum, axis=0)
    fresh = numer / (denom[:, None, :, None] + 1.0 / tau_power[None, None, :, None])
    return fresh.reshape(K, width), weight / IMGS, loglik
```

```python
import math

import jax
import jax.numpy as jnp
import numpy as np
from jax import lax
from jax.experimental import pallas as pl
from jax.experimental.pallas import tpu as pltpu
from jax.sharding import PartitionSpec as P

TRANS = 4
CYCLES = 32
ANG = 144
ROT = 36
NDEF = 16

STRIDE = ANG // ROT
HALF = STRIDE * CYCLES
LANES = 2 * HALF
REACH = 3
SIDE = 2 * REACH + 1
COMBOS = SIDE * SIDE
TABLE_ROWS = 112
BATCH = 4
HIGH = lax.Precision.HIGHEST
offset_sigma = 2.0


def phase_rows():
    turn = np.arange(ROT)[:, None, None]
    step = np.arange(STRIDE)[None, :, None]
    radius = np.arange(CYCLES)[None, None, :] + 1.0
    theta = 2.0 * math.pi * (STRIDE * turn + step) / ANG
    freq_x = (radius * np.cos(theta)).reshape(ROT, 1, HALF)
    freq_y = (radius * np.sin(theta)).reshape(ROT, 1, HALF)
    combo = np.arange(COMBOS)[None, :, None]
    dx = combo // SIDE - REACH
    dy = combo % SIDE - REACH
    angle = -2.0 * math.pi * (dx * freq_x + dy * freq_y) / (2.0 * CYCLES)
    full = np.concatenate([np.cos(angle), np.sin(angle)], axis=2)
    high = full.astype(jnp.bfloat16)
    low = (full - high.astype(np.float64)).astype(jnp.bfloat16)
    table = np.zeros((ROT, TABLE_ROWS, LANES), jnp.bfloat16)
    table[:, :COMBOS] = high
    table[:, COMBOS : 2 * COMBOS] = low
    return table


def turn_major(source):
    shaped = source.reshape(source.shape[0], 2, CYCLES, ROT, STRIDE)
    return shaped.transpose(3, 0, 1, 4, 2).reshape(ROT, source.shape[0], LANES)


def gather_kernel(n, own_ref, all_ref, send_sem, recv_sem, relay_send, relay_recv):
    me = lax.axis_index("img")
    partner = me + 1 - 2 * lax.rem(me, 2)
    peers = [lax.rem(me + 2 * hop, n) for hop in range(1, n // 2)]
    barrier = pltpu.get_barrier_semaphore()
    for peer in [partner] + peers:
        pl.semaphore_signal(
            barrier, inc=1, device_id={"img": peer}, device_id_type=pl.DeviceIdType.MESH
        )
    pl.semaphore_wait(barrier, n // 2)

    def send(src, dst, peer, left, landed):
        copy = pltpu.make_async_remote_copy(
            src_ref=src,
            dst_ref=dst,
            send_sem=left,
            recv_sem=landed,
            device_id={"img": peer},
            device_id_type=pl.DeviceIdType.MESH,
        )
        copy.start()
        return copy

    direct = [
        send(own_ref, all_ref.at[me], peer, send_sem.at[hop], recv_sem.at[hop])
        for hop, peer in enumerate(peers)
    ]
    relays = [send(own_ref, all_ref.at[me], partner, relay_send.at[0], relay_recv.at[0])]
    all_ref[me] = own_ref[...]
    for hop, copy in enumerate(direct):
        copy.wait_recv()
        source = lax.rem(me + n - 2 * (hop + 1), n)
        slot = all_ref.at[source]
        relays.append(
            send(slot, slot, partner, relay_send.at[hop + 1], relay_recv.at[hop + 1])
        )
    for copy in relays:
        copy.wait_recv()
    for copy in direct + relays:
        copy.wait_send()


def gather_images(own, n):
    return pl.pallas_call(
        lambda *refs: gather_kernel(n, *refs),
        out_shape=jax.ShapeDtypeStruct((n,) + own.shape, own.dtype),
        in_specs=[pl.BlockSpec(memory_space=pltpu.VMEM)],
        out_specs=pl.BlockSpec(memory_space=pltpu.VMEM),
        scratch_shapes=[
            pltpu.SemaphoreType.DMA((n // 2,)),
            pltpu.SemaphoreType.DMA((n // 2,)),
            pltpu.SemaphoreType.DMA((n // 2,)),
            pltpu.SemaphoreType.DMA((n // 2,)),
        ],
        compiler_params=pltpu.CompilerParams(collective_id=0, has_side_effects=True),
        name="gather_images",
    )(own)


def score_kernel(
    images_ref, refs_ref, prior_ref, ctf_ref, noise_ref, table_ref,
    ins_ref, expo_ref, stat_ref, square_ref, turned,
):
    n, _, local, _ = images_ref.shape
    owned = refs_ref.shape[1]
    count = n * local
    rows = count * TRANS
    height = ROT * owned
    for spot in range(2 * ROT):
        turned[spot * owned : (spot + 1) * owned] = refs_ref[-spot % ROT]
    meta = images_ref[:, ROT].astype(jnp.float32).reshape(count, LANES)
    group = lax.broadcasted_iota(jnp.int32, (count, NDEF), 1).astype(jnp.float32)
    chosen = (group == meta[:, :1]).astype(jnp.float32)
    contrast = jnp.dot(chosen, ctf_ref[...], precision=HIGH, preferred_element_type=jnp.float32)
    contrast = jnp.concatenate([contrast] * TRANS, axis=0)
    scaled = contrast / noise_ref[...]
    square = contrast * contrast
    square_ref[...] = square
    spot = lax.broadcasted_iota(jnp.int32, (count, TABLE_ROWS), 1).astype(jnp.float32)
    lane = lax.broadcasted_iota(jnp.int32, (count, HALF), 1)
    picks, offset_terms = [], []
    for t in range(TRANS):
        dx = meta[:, 1 + t : 2 + t]
        dy = meta[:, 1 + TRANS + t : 2 + TRANS + t]
        index = (dx + REACH) * SIDE + (dy + REACH)
        hit = (spot == index) | (spot == index + COMBOS)
        picks.append(hit.astype(jnp.float32).astype(jnp.bfloat16))
        value = -(dx * dx + dy * dy) / (2.0 * offset_sigma * offset_sigma)
        offset_terms.append(jnp.where(lane == 0, value, 0.0))
    pick = jnp.concatenate(picks, axis=0)
    offset_term = jnp.concatenate(offset_terms, axis=0)

    power = jnp.zeros((owned, HALF), jnp.float32)
    for b in range(ROT):
        entry = refs_ref[b].astype(jnp.float32)
        squares = entry * entry
        power = power + squares[:, :HALF] + squares[:, HALF:]
    by_lane = (((1,), (1,)), ((), ()))
    norm_coef = square / (2.0 * noise_ref[...])
    base = prior_ref[:, :1] - lax.dot_general(
        power, norm_coef, by_lane, precision=HIGH, preferred_element_type=jnp.float32
    )
    base = base + lax.dot_general(
        jnp.ones((owned, HALF), jnp.float32), offset_term, by_lane,
        precision=HIGH, preferred_element_type=jnp.float32,
    )

    for r in range(ROT):
        expo_ref[r * owned : (r + 1) * owned] = base

    @pl.loop(0, ROT // BATCH)
    def _(batch):
        left, right = [], []
        for part in range(BATCH):
            b = batch * BATCH + part
            phase = jnp.dot(pick, table_ref[b], preferred_element_type=jnp.float32)
            cosine, sine = phase[:, :HALF], phase[:, HALF:]
            picture = images_ref[:, b].astype(jnp.float32).reshape(count, LANES)
            picture = jnp.concatenate([picture] * TRANS, axis=0)
            real, imag = picture[:, :HALF], picture[:, HALF:]
            moved_real = real * cosine - imag * sine
            moved_imag = real * sine + imag * cosine
            ins_ref[b] = jnp.concatenate(
                [moved_real * contrast, moved_imag * contrast], axis=1
            ).astype(jnp.bfloat16)
            right.append(
                jnp.concatenate([moved_real * scaled, moved_imag * scaled], axis=1).astype(
                    jnp.bfloat16
                )
            )
            start = pl.multiple_of((ROT - b) * owned, owned)
            left.append(turned[pl.ds(start, height), :])
        expo_ref[...] += lax.dot_general(
            jnp.concatenate(left, axis=1), jnp.concatenate(right, axis=1), by_lane,
            preferred_element_type=jnp.float32,
        )

    logp = expo_ref[...]
    peak = jnp.max(logp, axis=0, keepdims=True)
    expo = jnp.exp(logp - peak)
    expo_ref[...] = expo
    stat_ref[0] = jnp.broadcast_to(peak, (8, rows))
    stat_ref[1] = jnp.broadcast_to(jnp.sum(expo, axis=0, keepdims=True), (8, rows))


def insert_kernel(
    stat_ref, expo_ref, ins_ref, square_ref, inv_tau_ref, fresh_ref, weight_ref, loglik_ref, turned
):
    rows = expo_ref.shape[1]
    height = expo_ref.shape[0]
    owned = height // ROT
    count = rows // TRANS
    peaks, sums = stat_ref[0], stat_ref[1]
    peak = jnp.broadcast_to(jnp.max(peaks, axis=0, keepdims=True), (8, rows))
    top = peak
    for t in range(1, TRANS):
        top = jnp.maximum(top, pltpu.roll(peak, t * count, 1))
    part = jnp.sum(sums * jnp.exp(peaks - top[:1]), axis=0, keepdims=True)
    part = jnp.broadcast_to(part, (8, rows))
    total = part
    for t in range(1, TRANS):
        total = total + pltpu.roll(part, t * count, 1)
    loglik_ref[...] = top + jnp.log(total)
    factor = jnp.exp(stat_ref[2][:1] - top[:1]) / total[:1]

    summed = jnp.zeros((owned, rows), jnp.float32)
    for r in range(ROT):
        post = (expo_ref[r * owned : (r + 1) * owned] * factor).astype(jnp.bfloat16)
        summed = summed + post.astype(jnp.float32)
        first = (ROT - r) % ROT
        for spot in (first, first + ROT):
            turned[spot * owned : (spot + 1) * owned] = post
    weight_ref[...] = jnp.broadcast_to(jnp.sum(summed, axis=1, keepdims=True), weight_ref.shape)
    denom = jnp.dot(summed, square_ref[...], precision=HIGH, preferred_element_type=jnp.float32)
    inverse = 1.0 / (denom + inv_tau_ref[...])
    inverse = jnp.concatenate([inverse, inverse], axis=1)

    fresh_ref[...] = jnp.zeros_like(fresh_ref)

    @pl.loop(0, ROT // BATCH)
    def _(batch):
        left, right = [], []
        for part_index in range(BATCH):
            s = batch * BATCH + part_index
            start = pl.multiple_of((ROT - s) * owned, owned)
            left.append(turned[pl.ds(start, height), :])
            right.append(ins_ref[s])
        fresh_ref[...] += jnp.dot(
            jnp.concatenate(left, axis=1), jnp.concatenate(right, axis=0),
            preferred_element_type=jnp.float32,
        )

    for b in range(ROT):
        block = pl.ds(b * owned, owned)
        fresh_ref[block] = fresh_ref[block] * inverse


def per_device(
    images, references, class_logprior, ctf_table, noise_power, tau_power, defocus, offsets
):
    n = lax.axis_size("img")
    local = images.shape[0]
    count = local * n
    rows = count * TRANS
    owned_true = references.shape[0]
    owned = -(-owned_true // 16) * 16
    spare = owned - owned_true
    vmem = pl.BlockSpec(memory_space=pltpu.VMEM)
    limit = 60 * 1024 * 1024

    moves = offsets.astype(jnp.float32)
    meta = jnp.concatenate(
        [defocus.astype(jnp.float32)[:, None], moves[..., 0], moves[..., 1]], axis=1
    )
    meta = jnp.pad(meta, ((0, 0), (0, LANES - meta.shape[1]))).astype(jnp.bfloat16)
    own = jnp.concatenate([turn_major(images), meta[None]], axis=0)
    gathered = gather_images(own, n)
    refs = jnp.pad(turn_major(references), ((0, 0), (0, spare), (0, 0)))
    prior = jnp.pad(class_logprior.astype(jnp.float32), (0, spare), constant_values=-1e30)
    prior = jnp.broadcast_to(prior[:, None], (owned, 128))

    inserted, expo, stat, square = pl.pallas_call(
        score_kernel,
        out_shape=(
            jax.ShapeDtypeStruct((ROT, rows, LANES), jnp.bfloat16),
            jax.ShapeDtypeStruct((ROT * owned, rows), jnp.float32),
            jax.ShapeDtypeStruct((2, 8, rows), jnp.float32),
            jax.ShapeDtypeStruct((rows, HALF), jnp.float32),
        ),
        in_specs=[vmem] * 6,
        out_specs=(vmem,) * 4,
        scratch_shapes=[pltpu.VMEM((2 * ROT * owned, LANES), jnp.bfloat16)],
        compiler_params=pltpu.CompilerParams(vmem_limit_bytes=limit),
        name="score",
    )(
        gathered,
        refs,
        prior,
        jnp.tile(ctf_table, (1, STRIDE)),
        jnp.tile(noise_power, STRIDE)[None],
        jnp.asarray(phase_rows()),
    )
    every = lax.all_gather(stat[:, 0], ("img", "cls"), axis=1)
    stats = jnp.concatenate(
        [every, jnp.broadcast_to(stat[:1, :1], (1,) + every.shape[1:])], axis=0
    )
    fresh, weight, loglik = pl.pallas_call(
        insert_kernel,
        out_shape=(
            jax.ShapeDtypeStruct((ROT * owned, LANES), jnp.float32),
            jax.ShapeDtypeStruct((owned, 128), jnp.float32),
            jax.ShapeDtypeStruct((8, rows), jnp.float32),
        ),
        in_specs=[vmem] * 5,
        out_specs=(vmem,) * 3,
        scratch_shapes=[pltpu.VMEM((2 * ROT * owned, rows), jnp.bfloat16)],
        compiler_params=pltpu.CompilerParams(vmem_limit_bytes=limit),
        name="insert",
    )(stats, expo, inserted, square, jnp.tile(1.0 / tau_power, STRIDE)[None])
    fresh = fresh.reshape(ROT, owned, 2, STRIDE, CYCLES)[:, :owned_true]
    fresh = fresh.transpose(1, 2, 4, 0, 3).reshape(owned_true, 2 * CYCLES * ANG)
    mine = lax.dynamic_slice_in_dim(loglik[0], lax.axis_index("img") * local, local, 0)
    return fresh, weight[:owned_true, 0] / count, mine


def solution(mesh):
    return jax.shard_map(
        per_device,
        mesh=mesh,
        in_specs=(
            P("img", None),
            P(("img", "cls"), None),
            P(("img", "cls")),
            P(),
            P(),
            P(),
            P("img"),
            P("img", None, None),
        ),
        out_specs=(P(("img", "cls"), None), P(("img", "cls")), P("img")),
        check_vma=False,
    )
```

```python
import math

import jax
import jax.numpy as jnp
import numpy as np
from jax import lax
from jax.experimental import pallas as pl
from jax.experimental.pallas import tpu as pltpu
from jax.sharding import PartitionSpec as P

TRANS = 4
CYCLES = 32
ANG = 144
ROT = 36
NDEF = 16

STRIDE = ANG // ROT
HALF = STRIDE * CYCLES
LANES = 2 * HALF
REACH = 3
SIDE = 2 * REACH + 1
COMBOS = SIDE * SIDE
TABLE_ROWS = 112
BATCH = 4
HIGH = lax.Precision.HIGHEST
offset_sigma = 2.0


def phase_rows():
    turn = np.arange(ROT)[:, None, None]
    step = np.arange(STRIDE)[None, :, None]
    radius = np.arange(CYCLES)[None, None, :] + 1.0
    theta = 2.0 * math.pi * (STRIDE * turn + step) / ANG
    freq_x = (radius * np.cos(theta)).reshape(ROT, 1, HALF)
    freq_y = (radius * np.sin(theta)).reshape(ROT, 1, HALF)
    combo = np.arange(COMBOS)[None, :, None]
    dx = combo // SIDE - REACH
    dy = combo % SIDE - REACH
    angle = -2.0 * math.pi * (dx * freq_x + dy * freq_y) / (2.0 * CYCLES)
    full = np.concatenate([np.cos(angle), np.sin(angle)], axis=2)
    high = full.astype(jnp.bfloat16)
    low = (full - high.astype(np.float64)).astype(jnp.bfloat16)
    table = np.zeros((ROT, TABLE_ROWS, LANES), jnp.bfloat16)
    table[:, :COMBOS] = high
    table[:, COMBOS : 2 * COMBOS] = low
    return table


def turn_major(source):
    shaped = source.reshape(source.shape[0], 2, CYCLES, ROT, STRIDE)
    return shaped.transpose(3, 0, 1, 4, 2).reshape(ROT, source.shape[0], LANES)


def gather_kernel(n, own_ref, all_ref, send_sem, recv_sem, relay_send, relay_recv):
    me = lax.axis_index("img")
    partner = me + 1 - 2 * lax.rem(me, 2)
    peers = [lax.rem(me + 2 * hop, n) for hop in range(1, n // 2)]
    barrier = pltpu.get_barrier_semaphore()
    for peer in [partner] + peers:
        pl.semaphore_signal(
            barrier, inc=1, device_id={"img": peer}, device_id_type=pl.DeviceIdType.MESH
        )
    pl.semaphore_wait(barrier, n // 2)

    def send(src, dst, peer, left, landed):
        copy = pltpu.make_async_remote_copy(
            src_ref=src,
            dst_ref=dst,
            send_sem=left,
            recv_sem=landed,
            device_id={"img": peer},
            device_id_type=pl.DeviceIdType.MESH,
        )
        copy.start()
        return copy

    direct = [
        send(own_ref, all_ref.at[me], peer, send_sem.at[hop], recv_sem.at[hop])
        for hop, peer in enumerate(peers)
    ]
    relays = [send(own_ref, all_ref.at[me], partner, relay_send.at[0], relay_recv.at[0])]
    all_ref[me] = own_ref[...]
    for hop, copy in enumerate(direct):
        copy.wait_recv()
        source = lax.rem(me + n - 2 * (hop + 1), n)
        slot = all_ref.at[source]
        relays.append(
            send(slot, slot, partner, relay_send.at[hop + 1], relay_recv.at[hop + 1])
        )
    for copy in relays:
        copy.wait_recv()
    for copy in direct + relays:
        copy.wait_send()


def gather_images(own, n):
    return pl.pallas_call(
        lambda *refs: gather_kernel(n, *refs),
        out_shape=jax.ShapeDtypeStruct((n,) + own.shape, own.dtype),
        in_specs=[pl.BlockSpec(memory_space=pltpu.VMEM)],
        out_specs=pl.BlockSpec(memory_space=pltpu.VMEM),
        scratch_shapes=[
            pltpu.SemaphoreType.DMA((n // 2,)),
            pltpu.SemaphoreType.DMA((n // 2,)),
            pltpu.SemaphoreType.DMA((n // 2,)),
            pltpu.SemaphoreType.DMA((n // 2,)),
        ],
        compiler_params=pltpu.CompilerParams(collective_id=0, has_side_effects=True),
        name="gather_images",
    )(own)


def exchange_kernel(n, m, own_ref, all_ref, local_sem, cls_send, cls_recv, img_send, img_recv):
    row, column = lax.axis_index("img"), lax.axis_index("cls")
    above = [{"cls": lax.rem(column + hop, m)} for hop in range(1, m)]
    beside = [{"img": lax.rem(row + hop, n)} for hop in range(1, n)]
    barrier = pltpu.get_barrier_semaphore()
    for peer in above + beside:
        pl.semaphore_signal(barrier, inc=1, device_id=peer, device_id_type=pl.DeviceIdType.MESH)
    pl.semaphore_wait(barrier, n + m - 2)

    def send_all(src, dst, peers, left, landed):
        copies = []
        for hop, peer in enumerate(peers):
            copy = pltpu.make_async_remote_copy(
                src_ref=src,
                dst_ref=dst,
                send_sem=left.at[hop],
                recv_sem=landed.at[hop],
                device_id=peer,
                device_id_type=pl.DeviceIdType.MESH,
            )
            copy.start()
            copies.append(copy)
        return copies

    slot = all_ref.at[row, column]
    first = send_all(own_ref, slot, above, cls_send, cls_recv)
    keep = pltpu.make_async_copy(own_ref, slot, local_sem)
    keep.start()
    keep.wait()
    for copy in first:
        copy.wait_recv()
    second = send_all(all_ref.at[row], all_ref.at[row], beside, img_send, img_recv)
    for copy in second:
        copy.wait_recv()
    for copy in first + second:
        copy.wait_send()


def exchange_stats(own, n, m):
    vmem = pl.BlockSpec(memory_space=pltpu.VMEM)
    return pl.pallas_call(
        lambda *refs: exchange_kernel(n, m, *refs),
        out_shape=jax.ShapeDtypeStruct((n, m) + own.shape, own.dtype),
        in_specs=[vmem],
        out_specs=vmem,
        scratch_shapes=[
            pltpu.SemaphoreType.DMA,
            pltpu.SemaphoreType.DMA((m,)),
            pltpu.SemaphoreType.DMA((m,)),
            pltpu.SemaphoreType.DMA((n,)),
            pltpu.SemaphoreType.DMA((n,)),
        ],
        compiler_params=pltpu.CompilerParams(collective_id=1, has_side_effects=True),
        name="exchange_stats",
    )(own)


def score_kernel(
    images_ref, refs_ref, prior_ref, ctf_ref, noise_ref, table_ref,
    ins_ref, expo_ref, stat_ref, square_ref, turned,
):
    n, _, local, _ = images_ref.shape
    owned = refs_ref.shape[1]
    count = n * local
    rows = count * TRANS
    height = ROT * owned
    for spot in range(2 * ROT):
        turned[spot * owned : (spot + 1) * owned] = refs_ref[-spot % ROT]
    meta = images_ref[:, ROT].astype(jnp.float32).reshape(count, LANES)
    group = lax.broadcasted_iota(jnp.int32, (count, NDEF), 1).astype(jnp.float32)
    chosen = (group == meta[:, :1]).astype(jnp.float32)
    contrast = jnp.dot(chosen, ctf_ref[...], precision=HIGH, preferred_element_type=jnp.float32)
    contrast = jnp.concatenate([contrast] * TRANS, axis=0)
    scaled = contrast / noise_ref[...]
    square = contrast * contrast
    square_ref[...] = square
    spot = lax.broadcasted_iota(jnp.int32, (count, TABLE_ROWS), 1).astype(jnp.float32)
    lane = lax.broadcasted_iota(jnp.int32, (count, HALF), 1)
    picks, offset_terms = [], []
    for t in range(TRANS):
        dx = meta[:, 1 + t : 2 + t]
        dy = meta[:, 1 + TRANS + t : 2 + TRANS + t]
        index = (dx + REACH) * SIDE + (dy + REACH)
        hit = (spot == index) | (spot == index + COMBOS)
        picks.append(hit.astype(jnp.float32).astype(jnp.bfloat16))
        value = -(dx * dx + dy * dy) / (2.0 * offset_sigma * offset_sigma)
        offset_terms.append(jnp.where(lane == 0, value, 0.0))
    pick = jnp.concatenate(picks, axis=0)
    offset_term = jnp.concatenate(offset_terms, axis=0)

    power = jnp.zeros((owned, HALF), jnp.float32)
    for b in range(ROT):
        entry = refs_ref[b].astype(jnp.float32)
        squares = entry * entry
        power = power + squares[:, :HALF] + squares[:, HALF:]
    by_lane = (((1,), (1,)), ((), ()))
    norm_coef = square / (2.0 * noise_ref[...])
    base = prior_ref[:, :1] - lax.dot_general(
        power, norm_coef, by_lane, precision=HIGH, preferred_element_type=jnp.float32
    )
    base = base + lax.dot_general(
        jnp.ones((owned, HALF), jnp.float32), offset_term, by_lane,
        precision=HIGH, preferred_element_type=jnp.float32,
    )

    for r in range(ROT):
        expo_ref[r * owned : (r + 1) * owned] = base

    @pl.loop(0, ROT // BATCH)
    def _(batch):
        left, right = [], []
        for part in range(BATCH):
            b = batch * BATCH + part
            phase = jnp.dot(pick, table_ref[b], preferred_element_type=jnp.float32)
            cosine, sine = phase[:, :HALF], phase[:, HALF:]
            picture = images_ref[:, b].astype(jnp.float32).reshape(count, LANES)
            picture = jnp.concatenate([picture] * TRANS, axis=0)
            real, imag = picture[:, :HALF], picture[:, HALF:]
            moved_real = real * cosine - imag * sine
            moved_imag = real * sine + imag * cosine
            ins_ref[b] = jnp.concatenate(
                [moved_real * contrast, moved_imag * contrast], axis=1
            ).astype(jnp.bfloat16)
            right.append(
                jnp.concatenate([moved_real * scaled, moved_imag * scaled], axis=1).astype(
                    jnp.bfloat16
                )
            )
            start = pl.multiple_of((ROT - b) * owned, owned)
            left.append(turned[pl.ds(start, height), :])
        expo_ref[...] += lax.dot_general(
            jnp.concatenate(left, axis=1), jnp.concatenate(right, axis=1), by_lane,
            preferred_element_type=jnp.float32,
        )

    logp = expo_ref[...]
    peak = jnp.max(logp, axis=0, keepdims=True)
    expo = jnp.exp(logp - peak)
    expo_ref[...] = expo
    which = lax.broadcasted_iota(jnp.int32, (8, rows), 0)
    stat_ref[...] = jnp.where(which == 0, peak, jnp.sum(expo, axis=0, keepdims=True))


def insert_kernel(
    every_ref, stat_ref, expo_ref, ins_ref, square_ref, inv_tau_ref, fresh_ref, weight_ref, loglik_ref, turned
):
    rows = expo_ref.shape[1]
    height = expo_ref.shape[0]
    owned = height // ROT
    count = rows // TRANS
    peaks, sums = every_ref[:, 0, :], every_ref[:, 1, :]
    peak = jnp.broadcast_to(jnp.max(peaks, axis=0, keepdims=True), (8, rows))
    top = peak
    for t in range(1, TRANS):
        top = jnp.maximum(top, pltpu.roll(peak, t * count, 1))
    part = jnp.sum(sums * jnp.exp(peaks - top[:1]), axis=0, keepdims=True)
    part = jnp.broadcast_to(part, (8, rows))
    total = part
    for t in range(1, TRANS):
        total = total + pltpu.roll(part, t * count, 1)
    loglik_ref[...] = top + jnp.log(total)
    factor = jnp.exp(stat_ref[:1] - top[:1]) / total[:1]

    summed = jnp.zeros((owned, rows), jnp.float32)
    for r in range(ROT):
        post = (expo_ref[r * owned : (r + 1) * owned] * factor).astype(jnp.bfloat16)
        summed = summed + post.astype(jnp.float32)
        first = (ROT - r) % ROT
        for spot in (first, first + ROT):
            turned[spot * owned : (spot + 1) * owned] = post
    weight_ref[...] = jnp.broadcast_to(jnp.sum(summed, axis=1, keepdims=True), weight_ref.shape)
    denom = jnp.dot(summed, square_ref[...], precision=HIGH, preferred_element_type=jnp.float32)
    inverse = 1.0 / (denom + inv_tau_ref[...])
    inverse = jnp.concatenate([inverse, inverse], axis=1)

    fresh_ref[...] = jnp.zeros_like(fresh_ref)

    @pl.loop(0, ROT // BATCH)
    def _(batch):
        left, right = [], []
        for part_index in range(BATCH):
            s = batch * BATCH + part_index
            start = pl.multiple_of((ROT - s) * owned, owned)
            left.append(turned[pl.ds(start, height), :])
            right.append(ins_ref[s])
        fresh_ref[...] += jnp.dot(
            jnp.concatenate(left, axis=1), jnp.concatenate(right, axis=0),
            preferred_element_type=jnp.float32,
        )

    for b in range(ROT):
        block = pl.ds(b * owned, owned)
        fresh_ref[block] = fresh_ref[block] * inverse


def per_device(
    images, references, class_logprior, ctf_table, noise_power, tau_power, defocus, offsets
):
    n = lax.axis_size("img")
    local = images.shape[0]
    count = local * n
    rows = count * TRANS
    owned_true = references.shape[0]
    owned = -(-owned_true // 16) * 16
    spare = owned - owned_true
    vmem = pl.BlockSpec(memory_space=pltpu.VMEM)
    limit = 60 * 1024 * 1024

    moves = offsets.astype(jnp.float32)
    meta = jnp.concatenate(
        [defocus.astype(jnp.float32)[:, None], moves[..., 0], moves[..., 1]], axis=1
    )
    meta = jnp.pad(meta, ((0, 0), (0, LANES - meta.shape[1]))).astype(jnp.bfloat16)
    own = jnp.concatenate([turn_major(images), meta[None]], axis=0)
    gathered = gather_images(own, n)
    refs = jnp.pad(turn_major(references), ((0, 0), (0, spare), (0, 0)))
    prior = jnp.pad(class_logprior.astype(jnp.float32), (0, spare), constant_values=-1e30)
    prior = jnp.broadcast_to(prior[:, None], (owned, 128))

    inserted, expo, stat, square = pl.pallas_call(
        score_kernel,
        out_shape=(
            jax.ShapeDtypeStruct((ROT, rows, LANES), jnp.bfloat16),
            jax.ShapeDtypeStruct((ROT * owned, rows), jnp.float32),
            jax.ShapeDtypeStruct((8, rows), jnp.float32),
            jax.ShapeDtypeStruct((rows, HALF), jnp.float32),
        ),
        in_specs=[vmem] * 6,
        out_specs=(vmem,) * 4,
        scratch_shapes=[pltpu.VMEM((2 * ROT * owned, LANES), jnp.bfloat16)],
        compiler_params=pltpu.CompilerParams(vmem_limit_bytes=limit),
        name="score",
    )(
        gathered,
        refs,
        prior,
        jnp.tile(ctf_table, (1, STRIDE)),
        jnp.tile(noise_power, STRIDE)[None],
        jnp.asarray(phase_rows()),
    )
    every = exchange_stats(stat, n, lax.axis_size("cls")).reshape(-1, 8, rows)
    fresh, weight, loglik = pl.pallas_call(
        insert_kernel,
        out_shape=(
            jax.ShapeDtypeStruct((ROT * owned, LANES), jnp.float32),
            jax.ShapeDtypeStruct((owned, 128), jnp.float32),
            jax.ShapeDtypeStruct((8, rows), jnp.float32),
        ),
        in_specs=[vmem] * 6,
        out_specs=(vmem,) * 3,
        scratch_shapes=[pltpu.VMEM((2 * ROT * owned, rows), jnp.bfloat16)],
        compiler_params=pltpu.CompilerParams(vmem_limit_bytes=limit),
        name="insert",
    )(every, stat, expo, inserted, square, jnp.tile(1.0 / tau_power, STRIDE)[None])
    fresh = fresh.reshape(ROT, owned, 2, STRIDE, CYCLES)[:, :owned_true]
    fresh = fresh.transpose(1, 2, 4, 0, 3).reshape(owned_true, 2 * CYCLES * ANG)
    mine = lax.dynamic_slice_in_dim(loglik[0], lax.axis_index("img") * local, local, 0)
    return fresh, weight[:owned_true, 0] / count, mine


def solution(mesh):
    return jax.shard_map(
        per_device,
        mesh=mesh,
        in_specs=(
            P("img", None),
            P(("img", "cls"), None),
            P(("img", "cls")),
            P(),
            P(),
            P(),
            P("img"),
            P("img", None, None),
        ),
        out_specs=(P(("img", "cls"), None), P(("img", "cls")), P("img")),
        check_vma=False,
    )
```
